32 devices in a mesh: ens: 2 (over x), gx: 16 (over z, y, core).
Axes of the slice: x: 2, y: 2, z: 4, core: 2. Of those that a mesh axis runs over, the one named last changes fastest.
Arguments:
- vectors: float32 [64, 64, 96, 128], P(None, ('ens', 'gx')), parts along dimension 1, may hold values from -45 to 45
- stream_speed: float32 [64, 96, 128], P(('ens', 'gx')), parts along dimension 0, may hold values from 0.5 to 1.5
- span_speed: float32 [64, 96, 128], P(('ens', 'gx')), parts along dimension 0, may hold values from -0.5 to 0.5
- damping: float32 [64, 96, 128], P(('ens', 'gx')), parts along dimension 0, may hold values from -0.5 to 0.5
Outputs:
- basis: float32 [64, 64, 96, 128], P(None, ('ens', 'gx')), parts along dimension 1
- growth: float32 [128], P('ens'), parts along dimension 0
The draws below stay inside these ranges and needn't reach their ends.
There are 2 independent parts, one for each index of `ens`. The reference program is written for one: setup_inputs(seed, part) draws one part's arguments, and reference() takes and returns one part's arrays. A program takes and returns all parts, laid end to end along the dimension named above; each array names one. Nothing has to cross between parts.
All inputs are finite; a program needn't handle non-finite values.
Results may differ from the reference program's by a relative error of at most 0.00055.
Values sent between devices are 32-bit elements; how exact they have to be, the bound alone decides.
No kernel may reach another device: no remote copies, remote signals or barrier semaphores. Data moves between devices by JAX's collectives and lax.ppermute only.
A program may use at most 256 MiB of HBM per device.

```python
import math
import jax
import jax.numpy as jnp
from jax import lax

VECS = 64
NY = 96
NZ = 128
NX = 32


def draw_vectors(key, part):
    key_base = jax.random.fold_in(key, 0)
    key_shared = jax.random.fold_in(key, 2)
    key_weight = jax.random.fold_in(key, 3)
    key_spread = jax.random.fold_in(key, 4)
    positions = jnp.arange(NX).astype(jnp.float32)
    envelope = (1.0 + 2.0 * positions / max(NX - 1, 1))[None, :, None, None]
    coupling = jax.random.uniform(key_weight, (VECS, 1, 1, 1), jnp.float32, 0.5, 1.5)
    spread = jnp.exp(jax.random.uniform(key_spread, (VECS, 1, 1, 1), jnp.float32, -3.912, -1.6094))
    raw_values = jnp.clip(jax.random.normal(key_base, (VECS, NX, NY, NZ), jnp.float32), -4.0, 4.0)
    shared = jnp.clip(jax.random.normal(key_shared, (1, NX, NY, NZ), jnp.float32), -4.0, 4.0)
    return ((coupling * shared + spread * raw_values) * envelope).astype(jnp.float32)


def block_levels(key, dims, shards, smallest, high):
    def one(dim, shards_of):
        draws = jax.random.uniform(jax.random.fold_in(jax.random.fold_in(key, 6), dim), (shards_of,), jnp.float32, smallest / len(shards), high / len(shards))
        return jnp.repeat(jnp.exp(draws), dims[dim] // shards_of).reshape((-1,) + (1,) * (len(dims) - dim - 1))

    factor_of = one(*shards[0])
    for cut in shards[1:]:
        factor_of = factor_of * one(*cut)
    return factor_of


def setup_inputs(seed: int = 0, part: int = 0) -> dict:
    streams_of = jax.random.split(jax.random.key(seed), 5)
    part_splits = jax.random.split(jax.random.fold_in(streams_of[4], part), 5)
    return {
        "vectors": draw_vectors(jax.random.fold_in(jax.random.fold_in(streams_of[4], part), 71), part),
        "stream_speed": jnp.clip(0.5 + 1.0 * jax.random.uniform(part_splits[1], (NX, NY, NZ), jnp.float32) ** block_levels(part_splits[1], (NX, NY, NZ), ((0, 16),), -0.2, 0.2), 0.5, 1.5),
        "span_speed": jnp.clip(jax.random.uniform(part_splits[2], (NX, NY, NZ), jnp.float32, -0.5, 0.5) * block_levels(part_splits[2], (NX, NY, NZ), ((0, 16),), -0.4, 0.0), -0.5, 0.5),
        "damping": jnp.clip(jax.random.uniform(part_splits[3], (NX, NY, NZ), jnp.float32, -0.5, 0.5) * block_levels(part_splits[3], (NX, NY, NZ), ((0, 16),), -0.4, 0.0), -0.5, 0.5),
    }


HIGH = lax.Precision.HIGHEST

def lower_solve(factor, values):
    return lax.linalg.triangular_solve(factor, values, left_side=True, lower=True)

def spectral_tables(points):
    indices = jnp.arange(points, dtype=jnp.int32)
    offset = indices[:, None] - indices[None, :]
    parity = (1 - 2 * ((offset + points) % 2)).astype(jnp.float32)
    spacing = 2.0 * math.pi / points
    diagonal_mask = offset == 0
    angles = jnp.where(diagonal_mask, 1, offset).astype(jnp.float32) * (spacing / 2.0)
    derivative = jnp.where(diagonal_mask, 0.0, 0.5 * parity * jnp.cos(angles) / jnp.sin(angles)) * spacing
    curvature = jnp.where(diagonal_mask, -math.pi ** 2 / 3.0 - spacing * spacing / 6.0, -parity / (2.0 * jnp.sin(angles) ** 2) * spacing * spacing)
    return jnp.concatenate([derivative.T, curvature.T], axis=1).astype(jnp.float32)

def operate(field, stream_speed, span_speed, damping, tables):
    points = field.shape[-1]
    forward = jnp.roll(field, -1, 0)
    behind = jnp.roll(field, 1, 0)
    walled = jnp.pad(field, ((0, 0), (1, 1), (0, 0)))
    lateral = walled[:, 2:] - 2.0 * field + walled[:, :-2]
    spanwise = jnp.dot(field.reshape(-1, points), tables, precision=HIGH).reshape(field.shape[:-1] + (2 * points,))
    return -stream_speed * (0.5 * (forward - behind)) - span_speed * spanwise[..., :points] + 0.05 * (forward - 2.0 * field + behind + lateral + spanwise[..., points:]) - damping * field

def reference(vectors, stream_speed, span_speed, damping):
    tables = spectral_tables(NZ)

    def advance(field):
        first = field + 0.3 * operate(field, stream_speed, span_speed, damping, tables)
        return 0.75 * field + 0.25 * (first + 0.3 * operate(first, stream_speed, span_speed, damping, tables))
    advanced = lax.map(advance, vectors)
    flattened = advanced.reshape(VECS, -1)
    total = jnp.float32(NX * NY * NZ)
    gram = jnp.dot(flattened, flattened.T, precision=HIGH) / total
    factor = jnp.linalg.cholesky(gram)
    partial_basis = lower_solve(factor, flattened)
    gram_second = jnp.dot(partial_basis, partial_basis.T, precision=HIGH) / total
    factor_second = jnp.linalg.cholesky(gram_second)
    basis = lower_solve(factor_second, partial_basis)
    growth = jnp.log(jnp.diagonal(factor)) + jnp.log(jnp.diagonal(factor_second))
    return (basis.reshape(vectors.shape), growth)
```

```python
import math

import jax
import jax.numpy as jnp
from jax import lax
from jax.sharding import PartitionSpec as P

HIGH = lax.Precision.HIGHEST


def shift(block, axis, step):
    count = lax.axis_size(axis)
    return lax.ppermute(block, axis, [(i, (i + step) % count) for i in range(count)])


def group_sum(value, axis):
    count = lax.axis_size(axis)
    if count & (count - 1):
        return lax.psum(value, axis)
    step = 1
    while step < count:
        value = value + lax.ppermute(value, axis, [(i, i ^ step) for i in range(count)])
        step *= 2
    return value


def spectral_tables(points):
    indices = jnp.arange(points, dtype=jnp.int32)
    offset = indices[:, None] - indices[None, :]
    parity = (1 - 2 * ((offset + points) % 2)).astype(jnp.float32)
    spacing = 2.0 * math.pi / points
    diagonal_mask = offset == 0
    angles = jnp.where(diagonal_mask, 1, offset).astype(jnp.float32) * (spacing / 2.0)
    derivative = (
        jnp.where(diagonal_mask, 0.0, 0.5 * parity * jnp.cos(angles) / jnp.sin(angles)) * spacing
    )
    curvature = jnp.where(
        diagonal_mask,
        -math.pi**2 / 3.0 - spacing * spacing / 6.0,
        -parity / (2.0 * jnp.sin(angles) ** 2) * spacing * spacing,
    )
    return jnp.concatenate([derivative.T, curvature.T], axis=1)


def operate(padded, coefficients, tables):
    stream_speed, span_speed, damping = coefficients
    points = padded.shape[-1]
    center = padded[:, 1:-1]
    forward = padded[:, 2:]
    behind = padded[:, :-2]
    walled = jnp.pad(center, ((0, 0), (0, 0), (1, 1), (0, 0)))
    lateral = walled[:, :, 2:] - 2.0 * center + walled[:, :, :-2]
    spanwise = jnp.dot(center.reshape(-1, points), tables, precision=HIGH).reshape(
        center.shape[:-1] + (2 * points,)
    )
    return (
        -stream_speed * (0.5 * (forward - behind))
        - span_speed * spanwise[..., :points]
        + 0.05 * (forward - 2.0 * center + behind + lateral + spanwise[..., points:])
        - damping * center
    )


def gram(values):
    return jnp.einsum("vpyz,upyz->vu", values, values, precision=HIGH)


def inverse(factor):
    return lax.linalg.triangular_solve(
        factor, jnp.eye(factor.shape[0], dtype=factor.dtype), left_side=True, lower=True
    )


def per_device(vectors, stream_speed, span_speed, damping):
    tables = spectral_tables(vectors.shape[-1])
    low = shift(vectors[:, -2:], "gx", 1)
    high = shift(vectors[:, :2], "gx", -1)
    coefficients = jnp.stack([stream_speed, span_speed, damping])
    coefficients = jnp.concatenate(
        [shift(coefficients[:, -1:], "gx", 1), coefficients, shift(coefficients[:, :1], "gx", -1)],
        axis=1,
    )
    total = jnp.float32(vectors[0].size * lax.axis_size("gx"))
    factor = jnp.linalg.cholesky(group_sum(gram(vectors), "gx") / total)
    mixer = inverse(factor)
    padded = jnp.concatenate([low, vectors, high], axis=1)
    first = padded[:, 1:-1] + 0.3 * operate(padded, coefficients, tables)
    advanced = 0.75 * vectors + 0.25 * (
        first[:, 1:-1] + 0.3 * operate(first, coefficients[:, 1:-1], tables)
    )
    partial_basis = jnp.einsum("vu,upyz->vpyz", mixer, advanced, precision=HIGH)
    factor_second = jnp.linalg.cholesky(group_sum(gram(partial_basis), "gx") / total)
    basis = jnp.einsum("vu,upyz->vpyz", inverse(factor_second), partial_basis, precision=HIGH)
    growth = jnp.log(jnp.diagonal(factor)) + jnp.log(jnp.diagonal(factor_second))
    return (basis, growth)


def solution(mesh):
    placed = (
        P(None, ("ens", "gx"), None, None),
        P(("ens", "gx"), None, None),
        P(("ens", "gx"), None, None),
        P(("ens", "gx"), None, None),
    )
    return jax.shard_map(
        per_device,
        mesh=mesh,
        in_specs=placed,
        out_specs=(P(None, ("ens", "gx"), None, None), P("ens")),
        check_vma=False,
    )
```

```python
import functools
import math

import jax
import jax.numpy as jnp
from jax import lax
from jax.experimental import pallas as pl
from jax.experimental.pallas import tpu as pltpu
from jax.sharding import PartitionSpec as P

HIGH = lax.Precision.HIGHEST
F32 = jnp.float32
BF16 = jnp.bfloat16
ROWS = 8
UNROLL = 8
FUSED = 6
HOP_EVERY = 1
STEP = 0.3
MIX = 0.05
VMEM_LIMIT = 24 * 1024 * 1024


def shift(block, axis, step):
    count = lax.axis_size(axis)
    return lax.ppermute(block, axis, [(i, (i + step) % count) for i in range(count)])


def exchange(value, axis, hop):
    return lax.ppermute(value, axis, [(i, i ^ hop) for i in range(lax.axis_size(axis))])


def group_sum(value, axis):
    hop = 1
    while hop < lax.axis_size(axis):
        value = value + exchange(value, axis, hop)
        hop *= 2
    return value


def spectral_tables(points):
    indices = jnp.arange(points, dtype=jnp.int32)
    offset = indices[:, None] - indices[None, :]
    parity = (1 - 2 * ((offset + points) % 2)).astype(F32)
    spacing = 2.0 * math.pi / points
    diagonal_mask = offset == 0
    angles = jnp.where(diagonal_mask, 1, offset).astype(F32) * (spacing / 2.0)
    derivative = (
        jnp.where(diagonal_mask, 0.0, 0.5 * parity * jnp.cos(angles) / jnp.sin(angles)) * spacing
    )
    curvature = jnp.where(
        diagonal_mask,
        -math.pi**2 / 3.0 - spacing * spacing / 6.0,
        -parity / (2.0 * jnp.sin(angles) ** 2) * spacing * spacing,
    )
    return jnp.concatenate([derivative.T, curvature.T], axis=1)


def pieces(value):
    high = value.astype(BF16)
    rest = value - high.astype(F32)
    middle = rest.astype(BF16)
    low = (rest - middle.astype(F32)).astype(BF16)
    return high, middle, low


def host_pieces(value):
    high = lax.reduce_precision(value, 8, 7)
    middle = lax.reduce_precision(value - high, 8, 7)
    low = (value - high) - middle
    return high.astype(BF16), middle.astype(BF16), low.astype(BF16)


def dot_nt(left, right, precision=None):
    return lax.dot_general(
        left, right, (((1,), (1,)), ((), ())), precision=precision, preferred_element_type=F32
    )


def repeat(start, stop, body):
    groups = (stop - start) // UNROLL
    if groups > 1:

        def several(group, carry):
            for inner in range(UNROLL):
                body(start + group * UNROLL + inner)
            return carry

        lax.fori_loop(0, groups, several, 0)
        start += groups * UNROLL
    for row in range(start, stop):
        body(row)


def turn_kernel(start, vectors_ref, turned_ref, block_ref, sem):
    count, planes, rows, points = block_ref.shape
    copy = pltpu.make_async_copy(vectors_ref.at[:, :, pl.ds(start, rows), :], block_ref, sem)
    copy.start()
    copy.wait()
    flat = block_ref.reshape(count * planes * rows, points)
    for row in range(rows):
        for plane in range(planes):
            turned_ref[plane, row] = flat[
                pl.ds(plane * rows + row, count, stride=planes * rows), :
            ]


def turn(vectors, start, rows):
    count, planes, height, points = vectors.shape
    return pl.pallas_call(
        functools.partial(turn_kernel, start),
        in_specs=[pl.BlockSpec(memory_space=pltpu.HBM)],
        out_specs=pl.BlockSpec(memory_space=pltpu.VMEM),
        scratch_shapes=[
            pltpu.VMEM((count, planes, rows, points), F32),
            pltpu.SemaphoreType.DMA,
        ],
        out_shape=jax.ShapeDtypeStruct((planes, rows, count, points), F32),
        compiler_params=pltpu.CompilerParams(vmem_limit_bytes=8 * 1024 * 1024),
        cost_estimate=pl.CostEstimate(
            flops=0, bytes_accessed=8 * count * planes * rows * points, transcendentals=0
        ),
        name="turn",
    )(vectors)


def gram_kernel(vectors_ref, gram_ref, slots, sems):
    count, planes, height, points = vectors_ref.shape
    steps = height // ROWS

    def fetch(step):
        return pltpu.make_async_copy(
            vectors_ref.at[:, :, pl.ds(pl.multiple_of(step * ROWS, ROWS), ROWS), :],
            slots.at[step % 2],
            sems.at[step % 2],
        )

    gram_ref[...] = jnp.zeros_like(gram_ref)
    fetch(0).start()

    def body(step, carry):
        @pl.when(step + 1 < steps)
        def _():
            fetch(step + 1).start()

        fetch(step).wait()
        flat = slots.at[step % 2].reshape(count * planes * ROWS, points)
        total = jnp.zeros((count, count), F32)
        for row in range(ROWS):
            both = jnp.concatenate(
                [
                    flat[pl.ds(plane * ROWS + row, count, stride=planes * ROWS), :]
                    for plane in range(planes)
                ],
                axis=1,
            )
            total += dot_nt(both, both, HIGH)
        gram_ref[...] += total
        return carry

    lax.fori_loop(0, steps, body, 0)


def gram_of(vectors):
    count, planes, height, points = vectors.shape
    return pl.pallas_call(
        gram_kernel,
        in_specs=[pl.BlockSpec(memory_space=pltpu.HBM)],
        out_specs=pl.BlockSpec(memory_space=pltpu.VMEM),
        out_shape=jax.ShapeDtypeStruct((count, count), F32),
        scratch_shapes=[
            pltpu.VMEM((2, count, planes, ROWS, points), F32),
            pltpu.SemaphoreType.DMA((2,)),
        ],
        compiler_params=pltpu.CompilerParams(vmem_limit_bytes=16 * 1024 * 1024),
        cost_estimate=pl.CostEstimate(
            flops=12 * vectors.size * count, bytes_accessed=4 * vectors.size, transcendentals=0
        ),
        name="gram",
    )(vectors)


def factor_body(gram):
    count = gram.shape[0]
    rows = lax.broadcasted_iota(jnp.int32, (count, count), 0)
    lanes = lax.broadcasted_iota(jnp.int32, (count, count), 1)
    work = jnp.concatenate([gram, jnp.where(rows == lanes, 1.0, 0.0).astype(F32)], axis=1)
    tile = 8
    blocks = [work[i : i + tile] for i in range(0, count, tile)]
    inverse_rows = []
    pivots = []
    for j in range(count):
        here, inner = divmod(j, tile)
        row = blocks[here][inner : inner + 1]
        pivot = row[:, j : j + 1]
        scale = lax.rsqrt(pivot)
        scaled = row * scale
        inverse_rows.append(scaled)
        pivots.append(pivot)
        row_all = jnp.broadcast_to(scaled, (tile, 2 * count))
        for b in range(here, len(blocks)):
            column = blocks[b][:, j : j + 1] * scale
            blocks[b] = blocks[b] - column * row_all
    inverse = jnp.concatenate(inverse_rows, axis=0)[:, count:]
    pivot = jnp.concatenate(pivots, axis=0)
    return inverse, 0.5 * jnp.log(pivot)


def factor_kernel(gram_ref, left_ref, logs_ref):
    inverse, logs = factor_body(gram_ref[...])
    left_ref[...] = split_six_left(inverse)
    logs_ref[...] = jnp.broadcast_to(logs, logs_ref.shape)


def factor(gram):
    count = gram.shape[0]
    return pl.pallas_call(
        factor_kernel,
        out_shape=[
            jax.ShapeDtypeStruct((count, 6 * count), BF16),
            jax.ShapeDtypeStruct((count, 128), F32),
        ],
        compiler_params=pltpu.CompilerParams(vmem_limit_bytes=4 * 1024 * 1024),
        name="factor",
    )(gram)


def split_six_right(value):
    high, middle, low = pieces(value)
    return jnp.concatenate([high, middle, high, middle, low, high], axis=0)


def split_six_left(value):
    high, middle, low = pieces(value)
    return jnp.concatenate([high, high, middle, middle, high, low], axis=1)


def mix_row(advanced, mixer_ref, basis_ref, row, gram_ref):
    points = advanced.shape[1] // 2
    mixed = jnp.dot(mixer_ref[...], split_six_right(advanced), preferred_element_type=F32)
    for plane in range(2):
        basis_ref[row, plane] = mixed[:, plane * points : (plane + 1) * points]
    high = mixed.astype(BF16)
    rest = (mixed - high.astype(F32)).astype(BF16)
    both = jnp.concatenate([high, rest], axis=0)
    gram_ref[...] += dot_nt(both, both)


def mix_kernel(rows, mixer_ref, _, basis_ref, gram_ref):
    gram_ref[...] = jnp.zeros_like(gram_ref)

    def body(row):
        advanced = jnp.concatenate([basis_ref[row, 0], basis_ref[row, 1]], axis=1)
        mix_row(advanced, mixer_ref, basis_ref, row, gram_ref)

    repeat(0, rows, body)


def mix(rows, mixer, basis):
    height, planes, count, points = basis.shape
    memory = pl.BlockSpec(memory_space=pltpu.VMEM)
    return pl.pallas_call(
        functools.partial(mix_kernel, rows),
        in_specs=[memory, memory],
        out_specs=[memory, memory],
        out_shape=[
            jax.ShapeDtypeStruct(basis.shape, F32),
            jax.ShapeDtypeStruct((2 * count, 2 * count), F32),
        ],
        input_output_aliases={1: 0},
        compiler_params=pltpu.CompilerParams(vmem_limit_bytes=8 * 1024 * 1024),
        cost_estimate=pl.CostEstimate(
            flops=rows * count * planes * points * count * 20,
            bytes_accessed=8 * rows * count * planes * points,
            transcendentals=0,
        ),
        name="mix",
    )(mixer, basis)


def advance_kernel(first, last, fused, base, *refs):
    refs = list(refs)
    tables_ref, coefs_ref, own_ref, low_ref, high_ref = refs[:5]
    refs = refs[5:]
    if not first:
        own_old_ref, low_old_ref, high_old_ref, state_in_ref, _ = refs[:5]
        refs = refs[5:]
    if fused:
        mixer_ref, gram_in_ref = refs[:2]
        refs = refs[2:]
    basis_ref = refs.pop(0)
    if not last:
        state_ref = refs.pop(0)
    if fused:
        gram_ref = refs.pop(0)
    field, stage, coef = refs
    rows, count, points = own_ref.shape[1:]
    start = 2 if first else 0
    stop = rows + 2 if last else rows
    zeros = jnp.zeros((count, points), F32)

    for plane in range(2):
        if first:
            for j in range(2):
                field[j, plane] = zeros
                field[j, 2 + plane] = zeros
                field[j, 4 + plane] = zeros
        else:
            field[0:2, plane] = low_old_ref[plane]
            field[0:2, 2 + plane] = own_old_ref[plane]
            field[0:2, 4 + plane] = high_old_ref[plane]
        field[2 : 2 + rows, plane] = low_ref[plane]
        field[2 : 2 + rows, 2 + plane] = own_ref[plane]
        field[2 : 2 + rows, 4 + plane] = high_ref[plane]
        if last:
            for q in range(3):
                field[2 + rows, 2 * q + plane] = zeros
    if first:
        for q in range(4):
            stage[2, q] = zeros
    else:
        stage[0:2] = state_in_ref[...]
        coef[0:2] = coefs_ref[base : base + 2]
    coef[2 : 2 + rows] = coefs_ref[base + 2 : base + 2 + rows]
    if last:
        for q in range(4):
            stage[rows + 3, q] = zeros
    if fused:
        gram_ref[...] = gram_in_ref[...]
    tables = tables_ref[...]

    def spanwise(values):
        high, middle, low = pieces(values)
        left = jnp.concatenate([high, middle, high, middle, low, high], axis=1)
        return jnp.dot(left, tables, preferred_element_type=F32)

    def slope(center, ahead, behind, above, below, product, row, q):
        c = coef[row, pl.ds(q * 4, 4), :]
        return (
            c[0:1] * ahead
            + c[1:2] * behind
            + c[2:3] * product[:, :points]
            + product[:, points:]
            + (STEP * MIX) * (above + below)
            + c[3:4] * center
        )

    def first_stage(i):
        middle_row = i - 1
        center = field[middle_row, 1:5].reshape(4 * count, points)
        product = spanwise(center)
        for q in range(4):
            mine = field[middle_row, 1 + q]
            stage[i, q] = mine + slope(
                mine,
                field[middle_row, 2 + q],
                field[middle_row, q],
                field[i, 1 + q],
                field[i - 2, 1 + q],
                product[q * count : (q + 1) * count],
                middle_row,
                q,
            )

    def second_stage(m):
        center = stage[m + 1, 1:3].reshape(2 * count, points)
        product = spanwise(center)
        results = []
        for q in range(1, 3):
            mine = stage[m + 1, q]
            value = mine + slope(
                mine,
                stage[m + 1, q + 1],
                stage[m + 1, q - 1],
                stage[m + 2, q],
                stage[m, q],
                product[(q - 1) * count : q * count],
                m,
                q,
            )
            results.append(0.75 * field[m, 1 + q] + 0.25 * value)
        if fused:
            mix_row(jnp.concatenate(results, axis=1), mixer_ref, basis_ref, base + m, gram_ref)
        else:
            for plane in range(2):
                basis_ref[base + m, plane] = results[plane]

    repeat(3 if first else 2, rows + 3 if last else rows + 2, first_stage)
    repeat(start, stop, second_stage)
    if not last:
        state_ref[...] = stage[rows : rows + 2]


def advance(index, base, height, tables, coefs, own, low, high, state, basis, mixer, gram):
    planes, rows, count, points = own[index].shape
    first, last, fused = index == 0, base + rows == height, gram is not None
    memory = pl.BlockSpec(memory_space=pltpu.VMEM)

    def whole(shape):
        return pl.BlockSpec(shape, lambda i: (0,) * len(shape))

    block = whole((planes, rows, count, points))
    before = 0 if first else own[index - 1].shape[1]
    tail = pl.BlockSpec((planes, 2, count, points), lambda i: (0, before // 2 - 1, 0, 0))
    operands = [tables, coefs, own[index], low[index], high[index]]
    specs = [memory, memory, block, block, block]
    aliases = {}
    if not first:
        operands += [own[index - 1], low[index - 1], high[index - 1], state, basis]
        specs += [tail, tail, tail, whole((2, 4, count, points)), memory]
        aliases = {len(operands) - 1: 0}
    out_specs = [memory]
    out_shape = [jax.ShapeDtypeStruct((height, planes, count, points), F32)]
    if not last:
        out_specs.append(whole((2, 4, count, points)))
        out_shape.append(jax.ShapeDtypeStruct((2, 4, count, points), F32))
    if fused:
        operands += [mixer, gram]
        specs += [memory, memory]
        out_specs.append(memory)
        out_shape.append(jax.ShapeDtypeStruct(gram.shape, F32))
    results = pl.pallas_call(
        functools.partial(advance_kernel, first, last, fused, base - 2),
        grid=(1,),
        in_specs=specs,
        out_specs=out_specs,
        out_shape=out_shape,
        scratch_shapes=[
            pltpu.VMEM((rows + 3, 6, count, points), F32),
            pltpu.VMEM((rows + 4, 4, count, points), F32),
            pltpu.VMEM((rows + 2, 16, points), F32),
        ],
        input_output_aliases=aliases,
        compiler_params=pltpu.CompilerParams(vmem_limit_bytes=VMEM_LIMIT),
        cost_estimate=pl.CostEstimate(
            flops=rows * count * points * 6 * 2 * 1000,
            bytes_accessed=4 * rows * count * points * 8,
            transcendentals=0,
        ),
        name="advance",
    )(*operands)
    results = list(results)
    basis = results.pop(0)
    state = None if last else results.pop(0)
    return basis, state, results[0] if fused else None


def finish_kernel(inverse_ref, partial_ref, basis_ref):
    count, planes, rows, points = basis_ref.shape
    start = pl.program_id(0) * rows
    flat = basis_ref.reshape(count * planes * rows, points)
    left = inverse_ref[:, : 4 * count]

    def body(row, carry):
        both = jnp.concatenate([partial_ref[start + row, 0], partial_ref[start + row, 1]], axis=1)
        upper = both.astype(BF16)
        lower = (both - upper.astype(F32)).astype(BF16)
        right = jnp.concatenate([upper, lower, upper, lower], axis=0)
        result = jnp.dot(left, right, preferred_element_type=F32)
        for plane in range(planes):
            flat[pl.ds(plane * rows + row, count, stride=planes * rows), :] = result[
                :, plane * points : (plane + 1) * points
            ]
        return carry

    lax.fori_loop(0, rows, body, 0, unroll=True)


def finish(inverse, partial_basis):
    height, planes, count, points = partial_basis.shape
    return pl.pallas_call(
        finish_kernel,
        grid=(height // ROWS,),
        in_specs=[
            pl.BlockSpec((count, 6 * count), lambda i: (0, 0)),
            pl.BlockSpec(memory_space=pltpu.VMEM),
        ],
        out_specs=pl.BlockSpec((count, planes, ROWS, points), lambda i: (0, 0, i, 0)),
        out_shape=jax.ShapeDtypeStruct((count, planes, height, points), F32),
        compiler_params=pltpu.CompilerParams(vmem_limit_bytes=VMEM_LIMIT),
        name="finish",
    )(inverse, partial_basis)


def chunk_rows(height):
    return [ROWS] * (height // ROWS)


def coefficient_rows(stream_speed, span_speed, damping):
    stacked = jnp.stack([stream_speed, span_speed, damping], axis=1)
    stream, span, damp = (
        lax.squeeze(part, [1])
        for part in jnp.split(
            jnp.concatenate(
                [shift(stacked[-1:], "gx", 1), stacked, shift(stacked[:1], "gx", -1)], axis=0
            ),
            3,
            axis=1,
        )
    )
    kinds = jnp.stack(
        [
            STEP * (MIX - 0.5 * stream),
            STEP * (MIX + 0.5 * stream),
            -STEP * span,
            -STEP * (4.0 * MIX + damp),
        ]
    )
    kinds = jnp.transpose(kinds, (2, 1, 0, 3))
    return kinds.reshape(kinds.shape[0], 16, kinds.shape[3])


def gated(value, gate):
    return lax.optimization_barrier((value, gate))[0]


def per_device(vectors, stream_speed, span_speed, damping):
    count, planes, height, points = vectors.shape
    members = lax.axis_size("gx")
    total = jnp.float32(planes * height * points * members)
    table = spectral_tables(points) * jnp.where(jnp.arange(2 * points) < points, 1.0, STEP * MIX)
    t_high, t_middle, t_low = host_pieces(table)
    tables = jnp.concatenate([t_high, t_high, t_middle, t_middle, t_high, t_low], axis=0)
    sizes = chunk_rows(height)
    starts = [sum(sizes[:index]) for index in range(len(sizes))]
    own, low, high = [], [], []

    def send(gate=None):
        index = len(own)
        if index == len(sizes):
            return
        turned = turn(vectors, starts[index], sizes[index])
        if gate is not None:
            turned = gated(turned, gate)
        own.append(turned)
        low.append(shift(turned, "gx", 1))
        high.append(shift(turned, "gx", -1))

    coefs = coefficient_rows(stream_speed, span_speed, damping)
    send()
    send()
    gram = gram_of(vectors)
    coefs = gated(coefs, gram)
    send(gram)
    hops = [1 << k for k in range((members - 1).bit_length())]
    mixer = mixed_gram = state = basis = None
    for index, start in enumerate(starts):
        if index == FUSED:
            for hop in hops:
                gram = gram + exchange(gram, "gx", hop)
            mixer, logs = factor(gram / total)
            basis, mixed_gram = mix(start - 2, mixer, basis)
        if 0 < index < FUSED and index % HOP_EVERY == 0:
            state = gated(state, gram)
        basis, state, mixed_gram = advance(
            index, start, height, tables, coefs, own, low, high, state, basis, mixer, mixed_gram
        )
        if index < FUSED and index % HOP_EVERY == 0 and hops:
            gram = gated(gram, state)
            gram = gram + exchange(gram, "gx", hops.pop(0))
        if state is not None:
            send(state)
    gram = mixed_gram
    gram = gram[:count, :count] + gram[:count, count:] + gram[count:, :count] + gram[count:, count:]
    inverse, logs_second = factor(group_sum(gram, "gx") / total)
    basis = finish(inverse, basis)
    growth = logs[:, 0] + logs_second[:, 0]
    return (basis, growth)


def solution(mesh):
    placed = (
        P(None, ("ens", "gx"), None, None),
        P(("ens", "gx"), None, None),
        P(("ens", "gx"), None, None),
        P(("ens", "gx"), None, None),
    )
    return jax.shard_map(
        per_device,
        mesh=mesh,
        in_specs=placed,
        out_specs=(P(None, ("ens", "gx"), None, None), P("ens")),
        check_vma=False,
    )
```

```python
import functools
import math

import jax
import jax.numpy as jnp
from jax import lax
from jax.experimental import pallas as pl
from jax.experimental.pallas import tpu as pltpu
from jax.sharding import PartitionSpec as P

HIGH = lax.Precision.HIGHEST
F32 = jnp.float32
BF16 = jnp.bfloat16
ROWS = 8
UNROLL = 8
FUSED = 5
HOP_EVERY = 1
STEP = 0.3
MIX = 0.05
VMEM_LIMIT = 24 * 1024 * 1024


def shift(block, axis, step):
    count = lax.axis_size(axis)
    return lax.ppermute(block, axis, [(i, (i + step) % count) for i in range(count)])


def exchange(value, axis, hop):
    return lax.ppermute(value, axis, [(i, i ^ hop) for i in range(lax.axis_size(axis))])


def group_sum(value, axis):
    hop = 1
    while hop < lax.axis_size(axis):
        value = value + exchange(value, axis, hop)
        hop *= 2
    return value


def spectral_tables(points):
    indices = jnp.arange(points, dtype=jnp.int32)
    offset = indices[:, None] - indices[None, :]
    parity = (1 - 2 * ((offset + points) % 2)).astype(F32)
    spacing = 2.0 * math.pi / points
    diagonal_mask = offset == 0
    angles = jnp.where(diagonal_mask, 1, offset).astype(F32) * (spacing / 2.0)
    derivative = (
        jnp.where(diagonal_mask, 0.0, 0.5 * parity * jnp.cos(angles) / jnp.sin(angles)) * spacing
    )
    curvature = jnp.where(
        diagonal_mask,
        -math.pi**2 / 3.0 - spacing * spacing / 6.0,
        -parity / (2.0 * jnp.sin(angles) ** 2) * spacing * spacing,
    )
    return jnp.concatenate([derivative.T, curvature.T], axis=1)


def pieces(value):
    high = value.astype(BF16)
    rest = value - high.astype(F32)
    middle = rest.astype(BF16)
    low = (rest - middle.astype(F32)).astype(BF16)
    return high, middle, low


def host_pieces(value):
    high = lax.reduce_precision(value, 8, 7)
    middle = lax.reduce_precision(value - high, 8, 7)
    low = (value - high) - middle
    return high.astype(BF16), middle.astype(BF16), low.astype(BF16)


def dot_nt(left, right, precision=None):
    return lax.dot_general(
        left, right, (((1,), (1,)), ((), ())), precision=precision, preferred_element_type=F32
    )


def repeat(start, stop, body):
    groups = (stop - start) // UNROLL
    if groups > 1:

        def several(group, carry):
            for inner in range(UNROLL):
                body(start + group * UNROLL + inner)
            return carry

        lax.fori_loop(0, groups, several, 0)
        start += groups * UNROLL
    for row in range(start, stop):
        body(row)


def turn_kernel(start, vectors_ref, turned_ref, block_ref, sem):
    count, planes, rows, points = block_ref.shape
    copy = pltpu.make_async_copy(vectors_ref.at[:, :, pl.ds(start, rows), :], block_ref, sem)
    copy.start()
    copy.wait()
    flat = block_ref.reshape(count * planes * rows, points)
    for row in range(rows):
        for plane in range(planes):
            turned_ref[plane, row] = flat[
                pl.ds(plane * rows + row, count, stride=planes * rows), :
            ]


def turn(vectors, start, rows):
    count, planes, height, points = vectors.shape
    return pl.pallas_call(
        functools.partial(turn_kernel, start),
        in_specs=[pl.BlockSpec(memory_space=pltpu.HBM)],
        out_specs=pl.BlockSpec(memory_space=pltpu.VMEM),
        scratch_shapes=[
            pltpu.VMEM((count, planes, rows, points), F32),
            pltpu.SemaphoreType.DMA,
        ],
        out_shape=jax.ShapeDtypeStruct((planes, rows, count, points), F32),
        compiler_params=pltpu.CompilerParams(vmem_limit_bytes=8 * 1024 * 1024),
        cost_estimate=pl.CostEstimate(
            flops=0, bytes_accessed=8 * count * planes * rows * points, transcendentals=0
        ),
        name="turn",
    )(vectors)


def gram_kernel(vectors_ref, gram_ref, slots, sems):
    count, planes, height, points = vectors_ref.shape
    steps = height // ROWS

    def fetch(step):
        return pltpu.make_async_copy(
            vectors_ref.at[:, :, pl.ds(pl.multiple_of(step * ROWS, ROWS), ROWS), :],
            slots.at[step % 2],
            sems.at[step % 2],
        )

    gram_ref[...] = jnp.zeros_like(gram_ref)
    fetch(0).start()

    def body(step, carry):
        @pl.when(step + 1 < steps)
        def _():
            fetch(step + 1).start()

        fetch(step).wait()
        flat = slots.at[step % 2].reshape(count * planes * ROWS, points)
        total = jnp.zeros((count, count), F32)
        for row in range(ROWS):
            both = jnp.concatenate(
                [
                    flat[pl.ds(plane * ROWS + row, count, stride=planes * ROWS), :]
                    for plane in range(planes)
                ],
                axis=1,
            )
            total += dot_nt(both, both, HIGH)
        gram_ref[...] += total
        return carry

    lax.fori_loop(0, steps, body, 0)


def gram_of(vectors):
    count, planes, height, points = vectors.shape
    return pl.pallas_call(
        gram_kernel,
        in_specs=[pl.BlockSpec(memory_space=pltpu.HBM)],
        out_specs=pl.BlockSpec(memory_space=pltpu.VMEM),
        out_shape=jax.ShapeDtypeStruct((count, count), F32),
        scratch_shapes=[
            pltpu.VMEM((2, count, planes, ROWS, points), F32),
            pltpu.SemaphoreType.DMA((2,)),
        ],
        compiler_params=pltpu.CompilerParams(vmem_limit_bytes=16 * 1024 * 1024),
        cost_estimate=pl.CostEstimate(
            flops=12 * vectors.size * count, bytes_accessed=4 * vectors.size, transcendentals=0
        ),
        name="gram",
    )(vectors)


def factor_kernel(scale, *refs):
    gram_ref, before_ref = refs[0], refs[1] if len(refs) > 4 else None
    left_ref, logs_ref, upper_ref = refs[-3:]
    count = gram_ref.shape[1]
    rows = lax.broadcasted_iota(jnp.int32, (count, count), 0)
    lanes = lax.broadcasted_iota(jnp.int32, (count, count), 1)
    tile = 8
    gram = gram_ref[...] * scale
    work = jnp.concatenate([gram, jnp.where(rows == lanes, 1.0, 0.0).astype(F32)], axis=1)
    blocks = [work[i : i + tile] for i in range(0, count, tile)]
    for j in range(count):
        here, inner = divmod(j, tile)
        row = blocks[here][inner : inner + 1]
        root = lax.rsqrt(row[:, j : j + 1])
        scaled = row * root
        upper_ref[j : j + 1, :] = scaled
        row_all = jnp.broadcast_to(scaled, (tile, 2 * count))
        for b in range(here, len(blocks)):
            blocks[b] = blocks[b] - (blocks[b][:, j : j + 1] * root) * row_all
    upper = upper_ref[...]
    left_ref[...] = split_six_left(upper[:, count:])
    diagonal = jnp.where(rows == lanes, upper[:, :count], 0.0)
    logs = jnp.log(jnp.sum(diagonal, axis=0, keepdims=True))
    logs_ref[...] = logs if before_ref is None else logs + before_ref[...]


def factor(gram, total, before=None):
    count = gram.shape[0]
    operands = [gram] + ([] if before is None else [before])
    return pl.pallas_call(
        functools.partial(factor_kernel, 1.0 / total),
        out_shape=[
            jax.ShapeDtypeStruct((count, 6 * count), BF16),
            jax.ShapeDtypeStruct((1, count), F32),
        ],
        scratch_shapes=[pltpu.VMEM((count, 2 * count), F32)],
        compiler_params=pltpu.CompilerParams(vmem_limit_bytes=4 * 1024 * 1024),
        name="factor",
    )(*operands)


def split_six_right(value):
    high, middle, low = pieces(value)
    return jnp.concatenate([high, middle, high, middle, low, high], axis=0)


def split_six_left(value):
    high, middle, low = pieces(value)
    return jnp.concatenate([high, high, middle, middle, high, low], axis=1)


def mix_kernel(start, stop, mixer_ref, _, *refs):
    basis_ref, gram_ref = refs[-2:]
    gram_ref[...] = refs[0][...] if len(refs) > 2 else jnp.zeros_like(gram_ref)
    points = basis_ref.shape[3]

    def group(first, rows):
        sides = []
        for row in range(rows):
            advanced = jnp.concatenate(
                [basis_ref[first + row, 0], basis_ref[first + row, 1]], axis=1
            )
            mixed = jnp.dot(
                mixer_ref[...], split_six_right(advanced), preferred_element_type=F32
            )
            for plane in range(2):
                basis_ref[first + row, plane] = mixed[:, plane * points : (plane + 1) * points]
            high = mixed.astype(BF16)
            rest = (mixed - high.astype(F32)).astype(BF16)
            sides.append(jnp.concatenate([high, rest], axis=0))
        sides = jnp.concatenate(sides, axis=1)
        gram_ref[...] += dot_nt(sides, sides)

    groups = (stop - start) // UNROLL
    if groups > 1:

        def several(index, carry):
            group(start + index * UNROLL, UNROLL)
            return carry

        lax.fori_loop(0, groups, several, 0)
        start += groups * UNROLL
    if stop > start:
        group(start, stop - start)


def mix(start, stop, mixer, basis, gram):
    height, planes, count, points = basis.shape
    memory = pl.BlockSpec(memory_space=pltpu.VMEM)
    operands = [mixer, basis] + ([] if gram is None else [gram])
    return pl.pallas_call(
        functools.partial(mix_kernel, start, stop),
        in_specs=[memory] * len(operands),
        out_specs=[memory, memory],
        out_shape=[
            jax.ShapeDtypeStruct(basis.shape, F32),
            jax.ShapeDtypeStruct((2 * count, 2 * count), F32),
        ],
        input_output_aliases={1: 0},
        compiler_params=pltpu.CompilerParams(vmem_limit_bytes=8 * 1024 * 1024),
        cost_estimate=pl.CostEstimate(
            flops=(stop - start) * count * planes * points * count * 20,
            bytes_accessed=8 * (stop - start) * count * planes * points,
            transcendentals=0,
        ),
        name="mix",
    )(*operands)


def advance_kernel(first, last, base, *refs):
    refs = list(refs)
    tables_ref, coefs_ref, own_ref, low_ref, high_ref = refs[:5]
    refs = refs[5:]
    if not first:
        own_old_ref, low_old_ref, high_old_ref, state_in_ref, _ = refs[:5]
        refs = refs[5:]
    basis_ref = refs.pop(0)
    if not last:
        state_ref = refs.pop(0)
    field, stage, coef = refs
    rows, count, points = own_ref.shape[1:]
    start = 2 if first else 0
    stop = rows + 2 if last else rows
    zeros = jnp.zeros((count, points), F32)

    for plane in range(2):
        if first:
            for j in range(2):
                field[j, plane] = zeros
                field[j, 2 + plane] = zeros
                field[j, 4 + plane] = zeros
        else:
            field[0:2, plane] = low_old_ref[plane]
            field[0:2, 2 + plane] = own_old_ref[plane]
            field[0:2, 4 + plane] = high_old_ref[plane]
        field[2 : 2 + rows, plane] = low_ref[plane]
        field[2 : 2 + rows, 2 + plane] = own_ref[plane]
        field[2 : 2 + rows, 4 + plane] = high_ref[plane]
        if last:
            for q in range(3):
                field[2 + rows, 2 * q + plane] = zeros
    if first:
        for q in range(4):
            stage[2, q] = zeros
    else:
        stage[0:2] = state_in_ref[...]
        coef[0:2] = coefs_ref[base : base + 2]
    coef[2 : 2 + rows] = coefs_ref[base + 2 : base + 2 + rows]
    if last:
        for q in range(4):
            stage[rows + 3, q] = zeros
    tables = tables_ref[...]

    def spanwise(values):
        high, middle, low = pieces(values)
        left = jnp.concatenate([high, middle, high, middle, low, high], axis=1)
        return jnp.dot(left, tables, preferred_element_type=F32)

    def slope(center, ahead, behind, above, below, product, row, q):
        c = coef[row, pl.ds(q * 4, 4), :]
        return (
            c[0:1] * ahead
            + c[1:2] * behind
            + c[2:3] * product[:, :points]
            + product[:, points:]
            + (STEP * MIX) * (above + below)
            + c[3:4] * center
        )

    def first_stage(i):
        middle_row = i - 1
        center = field[middle_row, 1:5].reshape(4 * count, points)
        product = spanwise(center)
        for q in range(4):
            mine = field[middle_row, 1 + q]
            stage[i, q] = mine + slope(
                mine,
                field[middle_row, 2 + q],
                field[middle_row, q],
                field[i, 1 + q],
                field[i - 2, 1 + q],
                product[q * count : (q + 1) * count],
                middle_row,
                q,
            )

    def second_stage(m):
        center = stage[m + 1, 1:3].reshape(2 * count, points)
        product = spanwise(center)
        results = []
        for q in range(1, 3):
            mine = stage[m + 1, q]
            value = mine + slope(
                mine,
                stage[m + 1, q + 1],
                stage[m + 1, q - 1],
                stage[m + 2, q],
                stage[m, q],
                product[(q - 1) * count : q * count],
                m,
                q,
            )
            results.append(0.75 * field[m, 1 + q] + 0.25 * value)
        for plane in range(2):
            basis_ref[base + m, plane] = results[plane]

    repeat(3 if first else 2, rows + 3 if last else rows + 2, first_stage)
    repeat(start, stop, second_stage)
    if not last:
        state_ref[...] = stage[rows : rows + 2]


def advance(index, base, height, tables, coefs, own, low, high, state, basis):
    planes, rows, count, points = own[index].shape
    first, last = index == 0, base + rows == height
    memory = pl.BlockSpec(memory_space=pltpu.VMEM)

    def whole(shape):
        return pl.BlockSpec(shape, lambda i: (0,) * len(shape))

    block = whole((planes, rows, count, points))
    before = 0 if first else own[index - 1].shape[1]
    tail = pl.BlockSpec((planes, 2, count, points), lambda i: (0, before // 2 - 1, 0, 0))
    operands = [tables, coefs, own[index], low[index], high[index]]
    specs = [memory, memory, block, block, block]
    aliases = {}
    if not first:
        operands += [own[index - 1], low[index - 1], high[index - 1], state, basis]
        specs += [tail, tail, tail, whole((2, 4, count, points)), memory]
        aliases = {len(operands) - 1: 0}
    out_specs = [memory]
    out_shape = [jax.ShapeDtypeStruct((height, planes, count, points), F32)]
    if not last:
        out_specs.append(whole((2, 4, count, points)))
        out_shape.append(jax.ShapeDtypeStruct((2, 4, count, points), F32))
    results = pl.pallas_call(
        functools.partial(advance_kernel, first, last, base - 2),
        grid=(1,),
        in_specs=specs,
        out_specs=out_specs,
        out_shape=out_shape,
        scratch_shapes=[
            pltpu.VMEM((rows + 3, 6, count, points), F32),
            pltpu.VMEM((rows + 4, 4, count, points), F32),
            pltpu.VMEM((rows + 2, 16, points), F32),
        ],
        input_output_aliases=aliases,
        compiler_params=pltpu.CompilerParams(vmem_limit_bytes=VMEM_LIMIT),
        cost_estimate=pl.CostEstimate(
            flops=rows * count * points * 6 * 2 * 1000,
            bytes_accessed=4 * rows * count * points * 8,
            transcendentals=0,
        ),
        name="advance",
    )(*operands)
    return results[0], None if last else results[1]


def finish_kernel(inverse_ref, partial_ref, basis_ref, slots, sems):
    _, planes, count, rows, points = slots.shape
    steps = partial_ref.shape[0] // rows
    left = inverse_ref[:, : 4 * count]

    def copies(step):
        return [
            pltpu.make_async_copy(
                slots.at[step % 2, plane],
                basis_ref.at[:, plane, pl.ds(pl.multiple_of(step * rows, 8), rows), :],
                sems.at[step % 2, plane],
            )
            for plane in range(planes)
        ]

    def body(step, carry):
        @pl.when(step >= 2)
        def _():
            for copy in copies(step - 2):
                copy.wait()

        flats = [
            slots.at[step % 2, plane].reshape(count * rows, points) for plane in range(planes)
        ]
        for row in range(rows):
            where = step * rows + row
            both = jnp.concatenate([partial_ref[where, 0], partial_ref[where, 1]], axis=1)
            upper = both.astype(BF16)
            lower = (both - upper.astype(F32)).astype(BF16)
            right = jnp.concatenate([upper, lower, upper, lower], axis=0)
            result = jnp.dot(left, right, preferred_element_type=F32)
            for plane in range(planes):
                flats[plane][pl.ds(row, count, stride=rows), :] = result[
                    :, plane * points : (plane + 1) * points
                ]
        for copy in copies(step):
            copy.start()
        return carry

    lax.fori_loop(0, steps, body, 0)
    for step in range(max(steps - 2, 0), steps):
        for copy in copies(step):
            copy.wait()


def finish(inverse, partial_basis):
    height, planes, count, points = partial_basis.shape
    rows = next(rows for rows in (24, 16, 8) if height % rows == 0)
    memory = pl.BlockSpec(memory_space=pltpu.VMEM)
    return pl.pallas_call(
        finish_kernel,
        in_specs=[memory, memory],
        out_specs=pl.BlockSpec(memory_space=pltpu.HBM),
        out_shape=jax.ShapeDtypeStruct((count, planes, height, points), F32),
        scratch_shapes=[
            pltpu.VMEM((2, planes, count, rows, points), F32),
            pltpu.SemaphoreType.DMA((2, planes)),
        ],
        compiler_params=pltpu.CompilerParams(vmem_limit_bytes=12 * 1024 * 1024),
        name="finish",
    )(inverse, partial_basis)


def chunk_rows(height):
    return [ROWS] * (height // ROWS)


def coefficient_rows(stream_speed, span_speed, damping):
    stacked = jnp.stack([stream_speed, span_speed, damping], axis=1)
    stream, span, damp = (
        lax.squeeze(part, [1])
        for part in jnp.split(
            jnp.concatenate(
                [shift(stacked[-1:], "gx", 1), stacked, shift(stacked[:1], "gx", -1)], axis=0
            ),
            3,
            axis=1,
        )
    )
    kinds = jnp.stack(
        [
            STEP * (MIX - 0.5 * stream),
            STEP * (MIX + 0.5 * stream),
            -STEP * span,
            -STEP * (4.0 * MIX + damp),
        ]
    )
    kinds = jnp.transpose(kinds, (2, 1, 0, 3))
    return kinds.reshape(kinds.shape[0], 16, kinds.shape[3])


def gated(value, gate):
    return lax.optimization_barrier((value, gate))[0]


def per_device(vectors, stream_speed, span_speed, damping):
    count, planes, height, points = vectors.shape
    members = lax.axis_size("gx")
    total = planes * height * points * members
    table = spectral_tables(points) * jnp.where(jnp.arange(2 * points) < points, 1.0, STEP * MIX)
    t_high, t_middle, t_low = host_pieces(table)
    tables = jnp.concatenate([t_high, t_high, t_middle, t_middle, t_high, t_low], axis=0)
    sizes = chunk_rows(height)
    starts = [sum(sizes[:index]) for index in range(len(sizes))]
    own, low, high = [], [], []

    def send(gate=None):
        index = len(own)
        if index == len(sizes):
            return
        turned = turn(vectors, starts[index], sizes[index])
        if gate is not None:
            turned = gated(turned, gate)
        own.append(turned)
        low.append(shift(turned, "gx", 1))
        high.append(shift(turned, "gx", -1))

    coefs = coefficient_rows(stream_speed, span_speed, damping)
    send()
    send()
    gram = gram_of(vectors)
    send(gram)
    hops = [1 << k for k in range((members - 1).bit_length())]
    gram = gram + exchange(gram, "gx", hops.pop(len(hops) > 1))
    coefs = gated(coefs, gram)
    mixed_gram = state = basis = None
    mixed = 0
    for index, start in enumerate(starts):
        if index == FUSED:
            for hop in hops:
                gram = gram + exchange(gram, "gx", hop)
            gram = gated(gram, state)
            mixer, logs = factor(gram, total)
        if 0 < index < FUSED and index % HOP_EVERY == 0:
            state = gated(state, gram)
        basis, state = advance(
            index, start, height, tables, coefs, own, low, high, state, basis
        )
        if index < FUSED and index % HOP_EVERY == 0 and hops:
            gram = gated(gram, state)
            gram = gram + exchange(gram, "gx", hops.pop(0))
        if index >= FUSED:
            ready = height if state is None else start + sizes[index] - 2
            basis, mixed_gram = mix(mixed, ready, mixer, basis, mixed_gram)
            mixed = ready
        if state is not None:
            send(state)
    gram = mixed_gram
    gram = gram[:count, :count] + gram[:count, count:] + gram[count:, :count] + gram[count:, count:]
    inverse, logs = factor(group_sum(gram, "gx"), total, logs)
    basis = finish(inverse, basis)
    growth = logs.reshape(count)
    return (basis, growth)


def solution(mesh):
    placed = (
        P(None, ("ens", "gx"), None, None),
        P(("ens", "gx"), None, None),
        P(("ens", "gx"), None, None),
        P(("ens", "gx"), None, None),
    )
    return jax.shard_map(
        per_device,
        mesh=mesh,
        in_specs=placed,
        out_specs=(P(None, ("ens", "gx"), None, None), P("ens")),
        check_vma=False,
    )
```

```python
import functools
import math

import jax
import jax.numpy as jnp
from jax import lax
from jax.experimental import pallas as pl
from jax.experimental.pallas import tpu as pltpu
from jax.sharding import PartitionSpec as P

HIGH = lax.Precision.HIGHEST
F32 = jnp.float32
BF16 = jnp.bfloat16
ROWS = 8
UNROLL = 8
PIVOTS = 4
FUSED = 5
HOP_EVERY = 1
STEP = 0.3
MIX = 0.05
VMEM_LIMIT = 24 * 1024 * 1024


def shift(block, axis, step):
    count = lax.axis_size(axis)
    return lax.ppermute(block, axis, [(i, (i + step) % count) for i in range(count)])


def exchange(value, axis, hop):
    return lax.ppermute(value, axis, [(i, i ^ hop) for i in range(lax.axis_size(axis))])


def group_sum(value, axis):
    hop = 1
    while hop < lax.axis_size(axis):
        value = value + exchange(value, axis, hop)
        hop *= 2
    return value


def spectral_tables(points):
    indices = jnp.arange(points, dtype=jnp.int32)
    offset = indices[:, None] - indices[None, :]
    parity = (1 - 2 * ((offset + points) % 2)).astype(F32)
    spacing = 2.0 * math.pi / points
    diagonal_mask = offset == 0
    angles = jnp.where(diagonal_mask, 1, offset).astype(F32) * (spacing / 2.0)
    derivative = (
        jnp.where(diagonal_mask, 0.0, 0.5 * parity * jnp.cos(angles) / jnp.sin(angles)) * spacing
    )
    curvature = jnp.where(
        diagonal_mask,
        -math.pi**2 / 3.0 - spacing * spacing / 6.0,
        -parity / (2.0 * jnp.sin(angles) ** 2) * spacing * spacing,
    )
    return jnp.concatenate([derivative.T, curvature.T], axis=1)


def pieces(value):
    high = value.astype(BF16)
    rest = value - high.astype(F32)
    middle = rest.astype(BF16)
    low = (rest - middle.astype(F32)).astype(BF16)
    return high, middle, low


def host_pieces(value):
    high = lax.reduce_precision(value, 8, 7)
    middle = lax.reduce_precision(value - high, 8, 7)
    low = (value - high) - middle
    return high.astype(BF16), middle.astype(BF16), low.astype(BF16)


def dot_nt(left, right, precision=None):
    return lax.dot_general(
        left, right, (((1,), (1,)), ((), ())), precision=precision, preferred_element_type=F32
    )


def repeat(start, stop, body):
    groups = (stop - start) // UNROLL
    if groups > 1:

        def several(group, carry):
            for inner in range(UNROLL):
                body(start + group * UNROLL + inner)
            return carry

        lax.fori_loop(0, groups, several, 0)
        start += groups * UNROLL
    for row in range(start, stop):
        body(row)


def turn_kernel(start, vectors_ref, turned_ref, block_ref, sem):
    count, planes, rows, points = block_ref.shape
    copy = pltpu.make_async_copy(vectors_ref.at[:, :, pl.ds(start, rows), :], block_ref, sem)
    copy.start()
    copy.wait()
    flat = block_ref.reshape(count * planes * rows, points)
    for row in range(rows):
        for plane in range(planes):
            turned_ref[plane, row] = flat[
                pl.ds(plane * rows + row, count, stride=planes * rows), :
            ]


def turn(vectors, start, rows):
    count, planes, height, points = vectors.shape
    return pl.pallas_call(
        functools.partial(turn_kernel, start),
        in_specs=[pl.BlockSpec(memory_space=pltpu.HBM)],
        out_specs=pl.BlockSpec(memory_space=pltpu.VMEM),
        scratch_shapes=[
            pltpu.VMEM((count, planes, rows, points), F32),
            pltpu.SemaphoreType.DMA,
        ],
        out_shape=jax.ShapeDtypeStruct((planes, rows, count, points), F32),
        compiler_params=pltpu.CompilerParams(vmem_limit_bytes=8 * 1024 * 1024),
        cost_estimate=pl.CostEstimate(
            flops=0, bytes_accessed=8 * count * planes * rows * points, transcendentals=0
        ),
        name="turn",
    )(vectors)


def gram_kernel(vectors_ref, gram_ref, slots, sems, acc):
    count, planes, height, points = vectors_ref.shape
    steps = height // ROWS

    def fetch(step):
        return pltpu.make_async_copy(
            vectors_ref.at[:, :, pl.ds(pl.multiple_of(step * ROWS, ROWS), ROWS), :],
            slots.at[step % 2],
            sems.at[step % 2],
        )

    acc[...] = jnp.zeros_like(acc)
    fetch(0).start()

    def body(step, carry):
        @pl.when(step + 1 < steps)
        def _():
            fetch(step + 1).start()

        fetch(step).wait()
        flat = slots.at[step % 2].reshape(count * planes * ROWS, points)
        total = jnp.zeros(acc.shape, F32)
        for row in range(ROWS):
            both = jnp.concatenate(
                [
                    flat[pl.ds(plane * ROWS + row, count, stride=planes * ROWS), :]
                    for plane in range(planes)
                ],
                axis=1,
            )
            split = jnp.concatenate(pieces(both), axis=0)
            total += dot_nt(split, split)
        acc[...] += total
        return carry

    lax.fori_loop(0, steps, body, 0)
    parts = [acc[k * count : (k + 1) * count, :] for k in range(3)]
    gram_ref[...] = (
        parts[0][:, :count]
        + (parts[0][:, count : 2 * count] + parts[1][:, :count])
        + (parts[1][:, count : 2 * count] + parts[0][:, 2 * count :] + parts[2][:, :count])
    )


def gram_of(vectors):
    count, planes, height, points = vectors.shape
    return pl.pallas_call(
        gram_kernel,
        in_specs=[pl.BlockSpec(memory_space=pltpu.HBM)],
        out_specs=pl.BlockSpec(memory_space=pltpu.VMEM),
        out_shape=jax.ShapeDtypeStruct((count, count), F32),
        scratch_shapes=[
            pltpu.VMEM((2, count, planes, ROWS, points), F32),
            pltpu.SemaphoreType.DMA((2,)),
            pltpu.VMEM((3 * count, 3 * count), F32),
        ],
        compiler_params=pltpu.CompilerParams(vmem_limit_bytes=16 * 1024 * 1024),
        cost_estimate=pl.CostEstimate(
            flops=12 * vectors.size * count, bytes_accessed=4 * vectors.size, transcendentals=0
        ),
        name="gram",
    )(vectors)


def factor_kernel(scale, *refs):
    gram_ref, before_ref = refs[0], refs[1] if len(refs) > 4 else None
    left_ref, logs_ref, upper_ref = refs[-3:]
    count = gram_ref.shape[1]
    rows = lax.broadcasted_iota(jnp.int32, (count, count), 0)
    lanes = lax.broadcasted_iota(jnp.int32, (count, count), 1)
    tile = 8
    gram = gram_ref[...] * scale
    work = jnp.concatenate([gram, jnp.where(rows == lanes, 1.0, 0.0).astype(F32)], axis=1)
    blocks = [work[i : i + tile] for i in range(0, count, tile)]
    for j in range(0, count, PIVOTS):
        here, inner = divmod(j, tile)
        spread = [
            [
                jnp.broadcast_to(blocks[b][:, j + q : j + q + 1], (tile, 2 * count))
                for q in range(PIVOTS)
            ]
            for b in range(here, len(blocks))
        ]
        lower = {}
        roots, scaled = [], []
        for q in range(PIVOTS):
            pivot = spread[0][q][inner + q : inner + q + 1]
            row = blocks[here][inner + q : inner + q + 1]
            for t in range(q):
                pivot = pivot - lower[q, t] * lower[q, t]
                row = row - lower[q, t] * scaled[t]
            roots.append(lax.rsqrt(pivot))
            scaled.append(row * roots[q])
            upper_ref[j + q : j + q + 1, :] = scaled[q]
            for p in range(q + 1, PIVOTS):
                entry = spread[0][q][inner + p : inner + p + 1]
                for t in range(q):
                    entry = entry - lower[p, t] * lower[q, t]
                lower[p, q] = entry * roots[q]
        for k, b in enumerate(range(here, len(blocks))):
            columns = []
            for q in range(PIVOTS):
                column = spread[k][q]
                for t in range(q):
                    column = column - columns[t] * lower[q, t]
                columns.append(column * roots[q])
                blocks[b] = blocks[b] - columns[q] * scaled[q]
    upper = upper_ref[...]
    left_ref[...] = split_six_left(upper[:, count:])
    diagonal = jnp.where(rows == lanes, upper[:, :count], 0.0)
    logs = jnp.log(jnp.sum(diagonal, axis=0, keepdims=True))
    logs_ref[...] = logs if before_ref is None else logs + before_ref[...]


def factor(gram, total, before=None):
    count = gram.shape[0]
    operands = [gram] + ([] if before is None else [before])
    return pl.pallas_call(
        functools.partial(factor_kernel, 1.0 / total),
        out_shape=[
            jax.ShapeDtypeStruct((count, 6 * count), BF16),
            jax.ShapeDtypeStruct((1, count), F32),
        ],
        scratch_shapes=[pltpu.VMEM((count, 2 * count), F32)],
        compiler_params=pltpu.CompilerParams(vmem_limit_bytes=4 * 1024 * 1024),
        name="factor",
    )(*operands)


def split_six_right(value):
    high, middle, low = pieces(value)
    return jnp.concatenate([high, middle, high, middle, low, high], axis=0)


def split_six_left(value):
    high, middle, low = pieces(value)
    return jnp.concatenate([high, high, middle, middle, high, low], axis=1)


def mix_kernel(start, stop, mixer_ref, _, *refs):
    basis_ref, gram_ref = refs[-2:]
    gram_ref[...] = refs[0][...] if len(refs) > 2 else jnp.zeros_like(gram_ref)
    points = basis_ref.shape[3]

    def group(first, rows):
        sides = []
        for row in range(rows):
            advanced = jnp.concatenate(
                [basis_ref[first + row, 0], basis_ref[first + row, 1]], axis=1
            )
            mixed = jnp.dot(
                mixer_ref[...], split_six_right(advanced), preferred_element_type=F32
            )
            for plane in range(2):
                basis_ref[first + row, plane] = mixed[:, plane * points : (plane + 1) * points]
            high = mixed.astype(BF16)
            rest = (mixed - high.astype(F32)).astype(BF16)
            sides.append(jnp.concatenate([high, rest], axis=0))
        sides = jnp.concatenate(sides, axis=1)
        gram_ref[...] += dot_nt(sides, sides)

    groups = (stop - start) // UNROLL
    if groups > 1:

        def several(index, carry):
            group(start + index * UNROLL, UNROLL)
            return carry

        lax.fori_loop(0, groups, several, 0)
        start += groups * UNROLL
    if stop > start:
        group(start, stop - start)


def mix(start, stop, mixer, basis, gram):
    height, planes, count, points = basis.shape
    memory = pl.BlockSpec(memory_space=pltpu.VMEM)
    operands = [mixer, basis] + ([] if gram is None else [gram])
    return pl.pallas_call(
        functools.partial(mix_kernel, start, stop),
        in_specs=[memory] * len(operands),
        out_specs=[memory, memory],
        out_shape=[
            jax.ShapeDtypeStruct(basis.shape, F32),
            jax.ShapeDtypeStruct((2 * count, 2 * count), F32),
        ],
        input_output_aliases={1: 0},
        compiler_params=pltpu.CompilerParams(vmem_limit_bytes=8 * 1024 * 1024),
        cost_estimate=pl.CostEstimate(
            flops=(stop - start) * count * planes * points * count * 20,
            bytes_accessed=8 * (stop - start) * count * planes * points,
            transcendentals=0,
        ),
        name="mix",
    )(*operands)


def advance_kernel(first, last, base, *refs):
    refs = list(refs)
    tables_ref, coefs_ref, own_ref, low_ref, high_ref = refs[:5]
    refs = refs[5:]
    if not first:
        own_old_ref, low_old_ref, high_old_ref, state_in_ref, _ = refs[:5]
        refs = refs[5:]
    basis_ref = refs.pop(0)
    if not last:
        state_ref = refs.pop(0)
    field, stage, coef = refs
    rows, count, points = own_ref.shape[1:]
    start = 2 if first else 0
    stop = rows + 2 if last else rows
    zeros = jnp.zeros((count, points), F32)

    for plane in range(2):
        if first:
            for j in range(2):
                field[j, plane] = zeros
                field[j, 2 + plane] = zeros
                field[j, 4 + plane] = zeros
        else:
            field[0:2, plane] = low_old_ref[plane]
            field[0:2, 2 + plane] = own_old_ref[plane]
            field[0:2, 4 + plane] = high_old_ref[plane]
        field[2 : 2 + rows, plane] = low_ref[plane]
        field[2 : 2 + rows, 2 + plane] = own_ref[plane]
        field[2 : 2 + rows, 4 + plane] = high_ref[plane]
        if last:
            for q in range(3):
                field[2 + rows, 2 * q + plane] = zeros
    if first:
        for q in range(4):
            stage[2, q] = zeros
    else:
        stage[0:2] = state_in_ref[...]
        coef[0:2] = coefs_ref[base : base + 2]
    coef[2 : 2 + rows] = coefs_ref[base + 2 : base + 2 + rows]
    if last:
        for q in range(4):
            stage[rows + 3, q] = zeros
    tables = tables_ref[...]

    def spanwise(values):
        high, middle, low = pieces(values)
        left = jnp.concatenate([high, middle, high, middle, low, high], axis=1)
        return jnp.dot(left, tables, preferred_element_type=F32)

    def slope(center, ahead, behind, above, below, product, row, q):
        c = coef[row, pl.ds(q * 4, 4), :]
        return (
            c[0:1] * ahead
            + c[1:2] * behind
            + c[2:3] * product[:, :points]
            + product[:, points:]
            + (STEP * MIX) * (above + below)
            + c[3:4] * center
        )

    def first_stage(i):
        middle_row = i - 1
        center = field[middle_row, 1:5].reshape(4 * count, points)
        product = spanwise(center)
        for q in range(4):
            mine = field[middle_row, 1 + q]
            stage[i, q] = mine + slope(
                mine,
                field[middle_row, 2 + q],
                field[middle_row, q],
                field[i, 1 + q],
                field[i - 2, 1 + q],
                product[q * count : (q + 1) * count],
                middle_row,
                q,
            )

    def second_stage(m):
        center = stage[m + 1, 1:3].reshape(2 * count, points)
        product = spanwise(center)
        results = []
        for q in range(1, 3):
            mine = stage[m + 1, q]
            value = mine + slope(
                mine,
                stage[m + 1, q + 1],
                stage[m + 1, q - 1],
                stage[m + 2, q],
                stage[m, q],
                product[(q - 1) * count : q * count],
                m,
                q,
            )
            results.append(0.75 * field[m, 1 + q] + 0.25 * value)
        for plane in range(2):
            basis_ref[base + m, plane] = results[plane]

    repeat(3 if first else 2, rows + 3 if last else rows + 2, first_stage)
    repeat(start, stop, second_stage)
    if not last:
        state_ref[...] = stage[rows : rows + 2]


def advance(index, base, height, tables, coefs, own, low, high, state, basis):
    planes, rows, count, points = own[index].shape
    first, last = index == 0, base + rows == height
    memory = pl.BlockSpec(memory_space=pltpu.VMEM)

    def whole(shape):
        return pl.BlockSpec(shape, lambda i: (0,) * len(shape))

    block = whole((planes, rows, count, points))
    before = 0 if first else own[index - 1].shape[1]
    tail = pl.BlockSpec((planes, 2, count, points), lambda i: (0, before // 2 - 1, 0, 0))
    operands = [tables, coefs, own[index], low[index], high[index]]
    specs = [memory, memory, block, block, block]
    aliases = {}
    if not first:
        operands += [own[index - 1], low[index - 1], high[index - 1], state, basis]
        specs += [tail, tail, tail, whole((2, 4, count, points)), memory]
        aliases = {len(operands) - 1: 0}
    out_specs = [memory]
    out_shape = [jax.ShapeDtypeStruct((height, planes, count, points), F32)]
    if not last:
        out_specs.append(whole((2, 4, count, points)))
        out_shape.append(jax.ShapeDtypeStruct((2, 4, count, points), F32))
    results = pl.pallas_call(
        functools.partial(advance_kernel, first, last, base - 2),
        grid=(1,),
        in_specs=specs,
        out_specs=out_specs,
        out_shape=out_shape,
        scratch_shapes=[
            pltpu.VMEM((rows + 3, 6, count, points), F32),
            pltpu.VMEM((rows + 4, 4, count, points), F32),
            pltpu.VMEM((rows + 2, 16, points), F32),
        ],
        input_output_aliases=aliases,
        compiler_params=pltpu.CompilerParams(vmem_limit_bytes=VMEM_LIMIT),
        cost_estimate=pl.CostEstimate(
            flops=rows * count * points * 6 * 2 * 1000,
            bytes_accessed=4 * rows * count * points * 8,
            transcendentals=0,
        ),
        name="advance",
    )(*operands)
    return results[0], None if last else results[1]


def finish_kernel(inverse_ref, partial_ref, basis_ref, slots, sems):
    _, planes, count, rows, points = slots.shape
    steps = partial_ref.shape[0] // rows
    left = inverse_ref[:, : 4 * count]

    def copies(step):
        return [
            pltpu.make_async_copy(
                slots.at[step % 2, plane],
                basis_ref.at[:, plane, pl.ds(pl.multiple_of(step * rows, 8), rows), :],
                sems.at[step % 2, plane],
            )
            for plane in range(planes)
        ]

    def body(step, carry):
        @pl.when(step >= 2)
        def _():
            for copy in copies(step - 2):
                copy.wait()

        flats = [
            slots.at[step % 2, plane].reshape(count * rows, points) for plane in range(planes)
        ]
        for row in range(rows):
            where = step * rows + row
            both = jnp.concatenate([partial_ref[where, 0], partial_ref[where, 1]], axis=1)
            upper = both.astype(BF16)
            lower = (both - upper.astype(F32)).astype(BF16)
            right = jnp.concatenate([upper, lower, upper, lower], axis=0)
            result = jnp.dot(left, right, preferred_element_type=F32)
            for plane in range(planes):
                flats[plane][pl.ds(row, count, stride=rows), :] = result[
                    :, plane * points : (plane + 1) * points
                ]
        for copy in copies(step):
            copy.start()
        return carry

    lax.fori_loop(0, steps, body, 0)
    for step in range(max(steps - 2, 0), steps):
        for copy in copies(step):
            copy.wait()


def finish(inverse, partial_basis):
    height, planes, count, points = partial_basis.shape
    rows = next(rows for rows in (24, 16, 8) if height % rows == 0)
    memory = pl.BlockSpec(memory_space=pltpu.VMEM)
    return pl.pallas_call(
        finish_kernel,
        in_specs=[memory, memory],
        out_specs=pl.BlockSpec(memory_space=pltpu.HBM),
        out_shape=jax.ShapeDtypeStruct((count, planes, height, points), F32),
        scratch_shapes=[
            pltpu.VMEM((2, planes, count, rows, points), F32),
            pltpu.SemaphoreType.DMA((2, planes)),
        ],
        compiler_params=pltpu.CompilerParams(vmem_limit_bytes=12 * 1024 * 1024),
        name="finish",
    )(inverse, partial_basis)


def chunk_rows(height):
    return [ROWS] * (height // ROWS)


def coefficient_rows(stream_speed, span_speed, damping):
    stacked = jnp.stack([stream_speed, span_speed, damping], axis=1)
    stream, span, damp = (
        lax.squeeze(part, [1])
        for part in jnp.split(
            jnp.concatenate(
                [shift(stacked[-1:], "gx", 1), stacked, shift(stacked[:1], "gx", -1)], axis=0
            ),
            3,
            axis=1,
        )
    )
    kinds = jnp.stack(
        [
            STEP * (MIX - 0.5 * stream),
            STEP * (MIX + 0.5 * stream),
            -STEP * span,
            -STEP * (4.0 * MIX + damp),
        ]
    )
    kinds = jnp.transpose(kinds, (2, 1, 0, 3))
    return kinds.reshape(kinds.shape[0], 16, kinds.shape[3])


def gated(value, gate):
    return lax.optimization_barrier((value, gate))[0]


def per_device(vectors, stream_speed, span_speed, damping):
    count, planes, height, points = vectors.shape
    members = lax.axis_size("gx")
    total = planes * height * points * members
    table = spectral_tables(points) * jnp.where(jnp.arange(2 * points) < points, 1.0, STEP * MIX)
    t_high, t_middle, t_low = host_pieces(table)
    tables = jnp.concatenate([t_high, t_high, t_middle, t_middle, t_high, t_low], axis=0)
    sizes = chunk_rows(height)
    starts = [sum(sizes[:index]) for index in range(len(sizes))]
    own, low, high = [], [], []

    def send(gate=None):
        index = len(own)
        if index == len(sizes):
            return
        turned = turn(vectors, starts[index], sizes[index])
        if gate is not None:
            turned = gated(turned, gate)
        own.append(turned)
        low.append(shift(turned, "gx", 1))
        high.append(shift(turned, "gx", -1))

    coefs = coefficient_rows(stream_speed, span_speed, damping)
    send()
    send()
    gram = gram_of(gated(vectors, own[1]))
    send(gram)
    hops = [1 << k for k in range((members - 1).bit_length())]
    gram = gram + exchange(gram, "gx", hops.pop(len(hops) > 1))
    coefs = gated(coefs, gram)
    mixed_gram = state = basis = None
    mixed = 0
    for index, start in enumerate(starts):
        if index == FUSED:
            for hop in hops:
                gram = gram + exchange(gram, "gx", hop)
            gram = gated(gram, state)
            mixer, logs = factor(gram, total)
        if 0 < index < FUSED and index % HOP_EVERY == 0:
            state = gated(state, gram)
        basis, state = advance(
            index, start, height, tables, coefs, own, low, high, state, basis
        )
        if index < FUSED and index % HOP_EVERY == 0 and hops:
            gram = gated(gram, state)
            gram = gram + exchange(gram, "gx", hops.pop(0))
        if index >= FUSED:
            ready = height if state is None else start + sizes[index] - 2
            basis, mixed_gram = mix(mixed, ready, mixer, basis, mixed_gram)
            mixed = ready
        if state is not None:
            send(state)
    gram = mixed_gram
    gram = gram[:count, :count] + gram[:count, count:] + gram[count:, :count] + gram[count:, count:]
    inverse, logs = factor(group_sum(gram, "gx"), total, logs)
    basis = finish(inverse, basis)
    growth = logs.reshape(count)
    return (basis, growth)


def solution(mesh):
    placed = (
        P(None, ("ens", "gx"), None, None),
        P(("ens", "gx"), None, None),
        P(("ens", "gx"), None, None),
        P(("ens", "gx"), None, None),
    )
    return jax.shard_map(
        per_device,
        mesh=mesh,
        in_specs=placed,
        out_specs=(P(None, ("ens", "gx"), None, None), P("ens")),
        check_vma=False,
    )
```

```python
import functools
import math

import jax
import jax.numpy as jnp
from jax import lax
from jax.experimental import pallas as pl
from jax.experimental.pallas import tpu as pltpu
from jax.sharding import PartitionSpec as P

HIGH = lax.Precision.HIGHEST
F32 = jnp.float32
BF16 = jnp.bfloat16
ROWS = 8
UNROLL = 8
PIVOTS = 8
FUSED = 5
HOP_EVERY = 1
STEP = 0.3
MIX = 0.05
VMEM_LIMIT = 24 * 1024 * 1024


def shift(block, axis, step):
    count = lax.axis_size(axis)
    return lax.ppermute(block, axis, [(i, (i + step) % count) for i in range(count)])


def exchange(value, axis, hop):
    return lax.ppermute(value, axis, [(i, i ^ hop) for i in range(lax.axis_size(axis))])


def group_sum(value, axis):
    hop = 1
    while hop < lax.axis_size(axis):
        value = value + exchange(value, axis, hop)
        hop *= 2
    return value


def spectral_tables(points):
    indices = jnp.arange(points, dtype=jnp.int32)
    offset = indices[:, None] - indices[None, :]
    parity = (1 - 2 * ((offset + points) % 2)).astype(F32)
    spacing = 2.0 * math.pi / points
    diagonal_mask = offset == 0
    angles = jnp.where(diagonal_mask, 1, offset).astype(F32) * (spacing / 2.0)
    derivative = (
        jnp.where(diagonal_mask, 0.0, 0.5 * parity * jnp.cos(angles) / jnp.sin(angles)) * spacing
    )
    curvature = jnp.where(
        diagonal_mask,
        -math.pi**2 / 3.0 - spacing * spacing / 6.0,
        -parity / (2.0 * jnp.sin(angles) ** 2) * spacing * spacing,
    )
    return jnp.concatenate([derivative.T, curvature.T], axis=1)


def pieces(value):
    high = value.astype(BF16)
    rest = value - high.astype(F32)
    middle = rest.astype(BF16)
    low = (rest - middle.astype(F32)).astype(BF16)
    return high, middle, low


def host_pieces(value):
    high = lax.reduce_precision(value, 8, 7)
    middle = lax.reduce_precision(value - high, 8, 7)
    low = (value - high) - middle
    return high.astype(BF16), middle.astype(BF16), low.astype(BF16)


def dot_nt(left, right, precision=None):
    return lax.dot_general(
        left, right, (((1,), (1,)), ((), ())), precision=precision, preferred_element_type=F32
    )


def repeat(start, stop, body):
    groups = (stop - start) // UNROLL
    if groups > 1:

        def several(group, carry):
            for inner in range(UNROLL):
                body(start + group * UNROLL + inner)
            return carry

        lax.fori_loop(0, groups, several, 0)
        start += groups * UNROLL
    for row in range(start, stop):
        body(row)


def turn_kernel(start, vectors_ref, turned_ref, block_ref, sem):
    count, planes, rows, points = block_ref.shape
    copy = pltpu.make_async_copy(vectors_ref.at[:, :, pl.ds(start, rows), :], block_ref, sem)
    copy.start()
    copy.wait()
    flat = block_ref.reshape(count * planes * rows, points)
    for row in range(rows):
        for plane in range(planes):
            turned_ref[plane, row] = flat[
                pl.ds(plane * rows + row, count, stride=planes * rows), :
            ]


def turn(vectors, start, rows):
    count, planes, height, points = vectors.shape
    return pl.pallas_call(
        functools.partial(turn_kernel, start),
        in_specs=[pl.BlockSpec(memory_space=pltpu.HBM)],
        out_specs=pl.BlockSpec(memory_space=pltpu.VMEM),
        scratch_shapes=[
            pltpu.VMEM((count, planes, rows, points), F32),
            pltpu.SemaphoreType.DMA,
        ],
        out_shape=jax.ShapeDtypeStruct((planes, rows, count, points), F32),
        compiler_params=pltpu.CompilerParams(vmem_limit_bytes=8 * 1024 * 1024),
        cost_estimate=pl.CostEstimate(
            flops=0, bytes_accessed=8 * count * planes * rows * points, transcendentals=0
        ),
        name="turn",
    )(vectors)


def gram_kernel(vectors_ref, gram_ref, slots, sems, acc):
    count, planes, height, points = vectors_ref.shape
    steps = height // ROWS

    def fetch(step):
        return pltpu.make_async_copy(
            vectors_ref.at[:, :, pl.ds(pl.multiple_of(step * ROWS, ROWS), ROWS), :],
            slots.at[step % 2],
            sems.at[step % 2],
        )

    acc[...] = jnp.zeros_like(acc)
    fetch(0).start()

    def body(step, carry):
        @pl.when(step + 1 < steps)
        def _():
            fetch(step + 1).start()

        fetch(step).wait()
        flat = slots.at[step % 2].reshape(count * planes * ROWS, points)
        total = jnp.zeros(acc.shape, F32)
        for row in range(ROWS):
            both = jnp.concatenate(
                [
                    flat[pl.ds(plane * ROWS + row, count, stride=planes * ROWS), :]
                    for plane in range(planes)
                ],
                axis=1,
            )
            split = jnp.concatenate(pieces(both), axis=0)
            total += dot_nt(split, split)
        acc[...] += total
        return carry

    lax.fori_loop(0, steps, body, 0)
    parts = [acc[k * count : (k + 1) * count, :] for k in range(3)]
    gram_ref[...] = (
        parts[0][:, :count]
        + (parts[0][:, count : 2 * count] + parts[1][:, :count])
        + (parts[1][:, count : 2 * count] + parts[0][:, 2 * count :] + parts[2][:, :count])
    )


def gram_of(vectors):
    count, planes, height, points = vectors.shape
    return pl.pallas_call(
        gram_kernel,
        in_specs=[pl.BlockSpec(memory_space=pltpu.HBM)],
        out_specs=pl.BlockSpec(memory_space=pltpu.VMEM),
        out_shape=jax.ShapeDtypeStruct((count, count), F32),
        scratch_shapes=[
            pltpu.VMEM((2, count, planes, ROWS, points), F32),
            pltpu.SemaphoreType.DMA((2,)),
            pltpu.VMEM((3 * count, 3 * count), F32),
        ],
        compiler_params=pltpu.CompilerParams(vmem_limit_bytes=16 * 1024 * 1024),
        cost_estimate=pl.CostEstimate(
            flops=12 * vectors.size * count, bytes_accessed=4 * vectors.size, transcendentals=0
        ),
        name="gram",
    )(vectors)


def factor_kernel(scale, *refs):
    gram_ref, before_ref = refs[0], refs[1] if len(refs) > 4 else None
    left_ref, logs_ref, upper_ref = refs[-3:]
    count = gram_ref.shape[1]
    rows = lax.broadcasted_iota(jnp.int32, (count, count), 0)
    lanes = lax.broadcasted_iota(jnp.int32, (count, count), 1)
    tile = 8
    gram = gram_ref[...] * scale
    work = jnp.concatenate([gram, jnp.where(rows == lanes, 1.0, 0.0).astype(F32)], axis=1)
    blocks = [work[i : i + tile] for i in range(0, count, tile)]
    for j in range(0, count, PIVOTS):
        here, inner = divmod(j, tile)
        spread = [
            [
                jnp.broadcast_to(blocks[b][:, j + q : j + q + 1], (tile, 2 * count))
                for q in range(PIVOTS)
            ]
            for b in range(here, len(blocks))
        ]
        lower = {}
        roots, scaled = [], []
        for q in range(PIVOTS):
            pivot = spread[0][q][inner + q : inner + q + 1]
            row = blocks[here][inner + q : inner + q + 1]
            for t in range(q):
                pivot = pivot - lower[q, t] * lower[q, t]
                row = row - lower[q, t] * scaled[t]
            roots.append(lax.rsqrt(pivot))
            scaled.append(row * roots[q])
            upper_ref[j + q : j + q + 1, :] = scaled[q]
            for p in range(q + 1, PIVOTS):
                entry = spread[0][q][inner + p : inner + p + 1]
                for t in range(q):
                    entry = entry - lower[p, t] * lower[q, t]
                lower[p, q] = entry * roots[q]
        for k, b in enumerate(range(here, len(blocks))):
            columns = []
            for q in range(PIVOTS):
                column = spread[k][q]
                for t in range(q):
                    column = column - columns[t] * lower[q, t]
                columns.append(column * roots[q])
                blocks[b] = blocks[b] - columns[q] * scaled[q]
    upper = upper_ref[...]
    left_ref[...] = split_six_left(upper[:, count:])
    diagonal = jnp.where(rows == lanes, upper[:, :count], 0.0)
    logs = jnp.log(jnp.sum(diagonal, axis=0, keepdims=True))
    logs_ref[...] = logs if before_ref is None else logs + before_ref[...]


def factor(gram, total, before=None):
    count = gram.shape[0]
    operands = [gram] + ([] if before is None else [before])
    return pl.pallas_call(
        functools.partial(factor_kernel, 1.0 / total),
        out_shape=[
            jax.ShapeDtypeStruct((count, 6 * count), BF16),
            jax.ShapeDtypeStruct((1, count), F32),
        ],
        scratch_shapes=[pltpu.VMEM((count, 2 * count), F32)],
        compiler_params=pltpu.CompilerParams(vmem_limit_bytes=4 * 1024 * 1024),
        name="factor",
    )(*operands)


def split_six_right(value):
    high, middle, low = pieces(value)
    return jnp.concatenate([high, middle, high, middle, low, high], axis=0)


def split_six_left(value):
    high, middle, low = pieces(value)
    return jnp.concatenate([high, high, middle, middle, high, low], axis=1)


def mix_kernel(start, stop, mixer_ref, _, *refs):
    basis_ref, gram_ref = refs[-2:]
    gram_ref[...] = refs[0][...] if len(refs) > 2 else jnp.zeros_like(gram_ref)
    points = basis_ref.shape[3]

    def group(first, rows):
        sides = []
        for row in range(rows):
            advanced = jnp.concatenate(
                [basis_ref[first + row, 0], basis_ref[first + row, 1]], axis=1
            )
            mixed = jnp.dot(
                mixer_ref[...], split_six_right(advanced), preferred_element_type=F32
            )
            for plane in range(2):
                basis_ref[first + row, plane] = mixed[:, plane * points : (plane + 1) * points]
            high = mixed.astype(BF16)
            rest = (mixed - high.astype(F32)).astype(BF16)
            sides.append(jnp.concatenate([high, rest], axis=0))
        sides = jnp.concatenate(sides, axis=1)
        gram_ref[...] += dot_nt(sides, sides)

    groups = (stop - start) // UNROLL
    if groups > 1:

        def several(index, carry):
            group(start + index * UNROLL, UNROLL)
            return carry

        lax.fori_loop(0, groups, several, 0)
        start += groups * UNROLL
    if stop > start:
        group(start, stop - start)


def mix(start, stop, mixer, basis, gram):
    height, planes, count, points = basis.shape
    memory = pl.BlockSpec(memory_space=pltpu.VMEM)
    operands = [mixer, basis] + ([] if gram is None else [gram])
    return pl.pallas_call(
        functools.partial(mix_kernel, start, stop),
        in_specs=[memory] * len(operands),
        out_specs=[memory, memory],
        out_shape=[
            jax.ShapeDtypeStruct(basis.shape, F32),
            jax.ShapeDtypeStruct((2 * count, 2 * count), F32),
        ],
        input_output_aliases={1: 0},
        compiler_params=pltpu.CompilerParams(vmem_limit_bytes=8 * 1024 * 1024),
        cost_estimate=pl.CostEstimate(
            flops=(stop - start) * count * planes * points * count * 20,
            bytes_accessed=8 * (stop - start) * count * planes * points,
            transcendentals=0,
        ),
        name="mix",
    )(*operands)


def advance_kernel(first, last, base, *refs):
    refs = list(refs)
    tables_ref, coefs_ref, own_ref, low_ref, high_ref = refs[:5]
    refs = refs[5:]
    if not first:
        own_old_ref, low_old_ref, high_old_ref, state_in_ref, _ = refs[:5]
        refs = refs[5:]
    basis_ref = refs.pop(0)
    if not last:
        state_ref = refs.pop(0)
    field, stage, coef = refs
    rows, count, points = own_ref.shape[1:]
    start = 2 if first else 0
    stop = rows + 2 if last else rows
    zeros = jnp.zeros((count, points), F32)

    for plane in range(2):
        if first:
            for j in range(2):
                field[j, plane] = zeros
                field[j, 2 + plane] = zeros
                field[j, 4 + plane] = zeros
        else:
            field[0:2, plane] = low_old_ref[plane]
            field[0:2, 2 + plane] = own_old_ref[plane]
            field[0:2, 4 + plane] = high_old_ref[plane]
        field[2 : 2 + rows, plane] = low_ref[plane]
        field[2 : 2 + rows, 2 + plane] = own_ref[plane]
        field[2 : 2 + rows, 4 + plane] = high_ref[plane]
        if last:
            for q in range(3):
                field[2 + rows, 2 * q + plane] = zeros
    if first:
        for q in range(4):
            stage[2, q] = zeros
    else:
        stage[0:2] = state_in_ref[...]
        coef[0:2] = coefs_ref[base : base + 2]
    coef[2 : 2 + rows] = coefs_ref[base + 2 : base + 2 + rows]
    if last:
        for q in range(4):
            stage[rows + 3, q] = zeros
    tables = tables_ref[...]

    def spanwise(values):
        high, middle, low = pieces(values)
        left = jnp.concatenate([high, middle, high, middle, low, high], axis=1)
        return jnp.dot(left, tables, preferred_element_type=F32)

    def slope(center, ahead, behind, above, below, product, row, q):
        c = coef[row, pl.ds(q * 4, 4), :]
        return (
            c[0:1] * ahead
            + c[1:2] * behind
            + c[2:3] * product[:, :points]
            + product[:, points:]
            + (STEP * MIX) * (above + below)
            + c[3:4] * center
        )

    def first_stage(i):
        middle_row = i - 1
        center = field[middle_row, 1:5].reshape(4 * count, points)
        product = spanwise(center)
        for q in range(4):
            mine = field[middle_row, 1 + q]
            stage[i, q] = mine + slope(
                mine,
                field[middle_row, 2 + q],
                field[middle_row, q],
                field[i, 1 + q],
                field[i - 2, 1 + q],
                product[q * count : (q + 1) * count],
                middle_row,
                q,
            )

    def second_stage(m):
        center = stage[m + 1, 1:3].reshape(2 * count, points)
        product = spanwise(center)
        results = []
        for q in range(1, 3):
            mine = stage[m + 1, q]
            value = mine + slope(
                mine,
                stage[m + 1, q + 1],
                stage[m + 1, q - 1],
                stage[m + 2, q],
                stage[m, q],
                product[(q - 1) * count : q * count],
                m,
                q,
            )
            results.append(0.75 * field[m, 1 + q] + 0.25 * value)
        for plane in range(2):
            basis_ref[base + m, plane] = results[plane]

    repeat(3 if first else 2, rows + 3 if last else rows + 2, first_stage)
    repeat(start, stop, second_stage)
    if not last:
        state_ref[...] = stage[rows : rows + 2]


def advance(index, base, height, tables, coefs, own, low, high, state, basis):
    planes, rows, count, points = own[index].shape
    first, last = index == 0, base + rows == height
    memory = pl.BlockSpec(memory_space=pltpu.VMEM)

    def whole(shape):
        return pl.BlockSpec(shape, lambda i: (0,) * len(shape))

    block = whole((planes, rows, count, points))
    before = 0 if first else own[index - 1].shape[1]
    tail = pl.BlockSpec((planes, 2, count, points), lambda i: (0, before // 2 - 1, 0, 0))
    operands = [tables, coefs, own[index], low[index], high[index]]
    specs = [memory, memory, block, block, block]
    aliases = {}
    if not first:
        operands += [own[index - 1], low[index - 1], high[index - 1], state, basis]
        specs += [tail, tail, tail, whole((2, 4, count, points)), memory]
        aliases = {len(operands) - 1: 0}
    out_specs = [memory]
    out_shape = [jax.ShapeDtypeStruct((height, planes, count, points), F32)]
    if not last:
        out_specs.append(whole((2, 4, count, points)))
        out_shape.append(jax.ShapeDtypeStruct((2, 4, count, points), F32))
    results = pl.pallas_call(
        functools.partial(advance_kernel, first, last, base - 2),
        grid=(1,),
        in_specs=specs,
        out_specs=out_specs,
        out_shape=out_shape,
        scratch_shapes=[
            pltpu.VMEM((rows + 3, 6, count, points), F32),
            pltpu.VMEM((rows + 4, 4, count, points), F32),
            pltpu.VMEM((rows + 2, 16, points), F32),
        ],
        input_output_aliases=aliases,
        compiler_params=pltpu.CompilerParams(vmem_limit_bytes=VMEM_LIMIT),
        cost_estimate=pl.CostEstimate(
            flops=rows * count * points * 6 * 2 * 1000,
            bytes_accessed=4 * rows * count * points * 8,
            transcendentals=0,
        ),
        name="advance",
    )(*operands)
    return results[0], None if last else results[1]


def finish_kernel(inverse_ref, partial_ref, basis_ref, slots, sems):
    _, planes, count, rows, points = slots.shape
    steps = partial_ref.shape[0] // rows
    left = inverse_ref[:, : 4 * count]

    def copies(step):
        return [
            pltpu.make_async_copy(
                slots.at[step % 2, plane],
                basis_ref.at[:, plane, pl.ds(pl.multiple_of(step * rows, 8), rows), :],
                sems.at[step % 2, plane],
            )
            for plane in range(planes)
        ]

    def body(step, carry):
        @pl.when(step >= 2)
        def _():
            for copy in copies(step - 2):
                copy.wait()

        flats = [
            slots.at[step % 2, plane].reshape(count * rows, points) for plane in range(planes)
        ]
        for row in range(rows):
            where = step * rows + row
            both = jnp.concatenate([partial_ref[where, 0], partial_ref[where, 1]], axis=1)
            upper = both.astype(BF16)
            lower = (both - upper.astype(F32)).astype(BF16)
            right = jnp.concatenate([upper, lower, upper, lower], axis=0)
            result = jnp.dot(left, right, preferred_element_type=F32)
            for plane in range(planes):
                flats[plane][pl.ds(row, count, stride=rows), :] = result[
                    :, plane * points : (plane + 1) * points
                ]
        for copy in copies(step):
            copy.start()
        return carry

    lax.fori_loop(0, steps, body, 0)
    for step in range(max(steps - 2, 0), steps):
        for copy in copies(step):
            copy.wait()


def finish(inverse, partial_basis):
    height, planes, count, points = partial_basis.shape
    rows = next(rows for rows in (24, 16, 8) if height % rows == 0)
    memory = pl.BlockSpec(memory_space=pltpu.VMEM)
    return pl.pallas_call(
        finish_kernel,
        in_specs=[memory, memory],
        out_specs=pl.BlockSpec(memory_space=pltpu.HBM),
        out_shape=jax.ShapeDtypeStruct((count, planes, height, points), F32),
        scratch_shapes=[
            pltpu.VMEM((2, planes, count, rows, points), F32),
            pltpu.SemaphoreType.DMA((2, planes)),
        ],
        compiler_params=pltpu.CompilerParams(vmem_limit_bytes=12 * 1024 * 1024),
        name="finish",
    )(inverse, partial_basis)


def chunk_rows(height):
    return [ROWS] * (height // ROWS)


def coefficient_rows(stream_speed, span_speed, damping):
    stacked = jnp.stack([stream_speed, span_speed, damping], axis=1)
    stream, span, damp = (
        lax.squeeze(part, [1])
        for part in jnp.split(
            jnp.concatenate(
                [shift(stacked[-1:], "gx", 1), stacked, shift(stacked[:1], "gx", -1)], axis=0
            ),
            3,
            axis=1,
        )
    )
    kinds = jnp.stack(
        [
            STEP * (MIX - 0.5 * stream),
            STEP * (MIX + 0.5 * stream),
            -STEP * span,
            -STEP * (4.0 * MIX + damp),
        ]
    )
    kinds = jnp.transpose(kinds, (2, 1, 0, 3))
    return kinds.reshape(kinds.shape[0], 16, kinds.shape[3])


def gated(value, gate):
    return lax.optimization_barrier((value, gate))[0]


def per_device(vectors, stream_speed, span_speed, damping):
    count, planes, height, points = vectors.shape
    members = lax.axis_size("gx")
    total = planes * height * points * members
    table = spectral_tables(points) * jnp.where(jnp.arange(2 * points) < points, 1.0, STEP * MIX)
    t_high, t_middle, t_low = host_pieces(table)
    tables = jnp.concatenate([t_high, t_high, t_middle, t_middle, t_high, t_low], axis=0)
    sizes = chunk_rows(height)
    starts = [sum(sizes[:index]) for index in range(len(sizes))]
    own, low, high = [], [], []

    def send(gate=None):
        index = len(own)
        if index == len(sizes):
            return
        turned = turn(vectors, starts[index], sizes[index])
        if gate is not None:
            turned = gated(turned, gate)
        own.append(turned)
        low.append(shift(turned, "gx", 1))
        high.append(shift(turned, "gx", -1))

    coefs = coefficient_rows(stream_speed, span_speed, damping)
    send()
    send()
    gram = gram_of(gated(vectors, own[1]))
    send(gram)
    hops = [1 << k for k in range((members - 1).bit_length())]
    gram = gram + exchange(gram, "gx", hops.pop(len(hops) > 1))
    coefs = gated(coefs, gram)
    mixed_gram = state = basis = None
    mixed = 0
    for index, start in enumerate(starts):
        if index == FUSED:
            for hop in hops:
                gram = gram + exchange(gram, "gx", hop)
            gram = gated(gram, state)
            mixer, logs = factor(gram, total)
        if 0 < index < FUSED and index % HOP_EVERY == 0:
            state = gated(state, gram)
        basis, state = advance(
            index, start, height, tables, coefs, own, low, high, state, basis
        )
        if index < FUSED and index % HOP_EVERY == 0 and hops:
            gram = gated(gram, state)
            gram = gram + exchange(gram, "gx", hops.pop(0))
        if index >= FUSED:
            ready = height if state is None else start + sizes[index] - 2
            basis, mixed_gram = mix(mixed, ready, mixer, basis, mixed_gram)
            mixed = ready
        if state is not None:
            send(state)
    gram = mixed_gram
    gram = gram[:count, :count] + gram[:count, count:] + gram[count:, :count] + gram[count:, count:]
    inverse, logs = factor(group_sum(gram, "gx"), total, logs)
    basis = finish(inverse, basis)
    growth = logs.reshape(count)
    return (basis, growth)


def solution(mesh):
    placed = (
        P(None, ("ens", "gx"), None, None),
        P(("ens", "gx"), None, None),
        P(("ens", "gx"), None, None),
        P(("ens", "gx"), None, None),
    )
    return jax.shard_map(
        per_device,
        mesh=mesh,
        in_specs=placed,
        out_specs=(P(None, ("ens", "gx"), None, None), P("ens")),
        check_vma=False,
    )
```
